32 devices in a mesh: wide: 8 (over z, x), narrow: 4 (over y, core).
Axes of the slice: x: 2, y: 2, z: 4, core: 2. Of those that a mesh axis runs over, the one named last changes fastest.
Arguments:
- dens_tiles: bfloat16 [512, 3, 128, 128], P(('wide', 'narrow')), may hold values from -6 to 6
- tile_dest: int32 [512, 2], P(('wide', 'narrow')), may hold values from 0 to 7, all different within a row; in each aligned block of 16 rows (0 to 15, 16 to 31, ...) at most 8 rows name the same one
- tile_place: int32 [512, 2], P(('wide', 'narrow')), may hold values from 0 to 49
- tile_rows: int32 [512], P(('wide', 'narrow')), may hold values from 0 to 15
- tile_cols: int32 [512], P(('wide', 'narrow')), may hold values from 0 to 31
- ao_values: bfloat16 [16, 640, 1280], P('wide'), may hold values from -0.25 to 0.25
- point_count: int32 [16], P('wide'), may hold values from 1 to 1280, 12800 in all
- weights: float32 [16, 1280], P('wide'), may hold values from 0.05 to 1
- kernel_first: float32 [16, 1280], P('wide'), may hold values from -1.5 to -0.3
- kernel_second: float32 [16, 1280], P('wide'), may hold values from 0.2 to 2
- occ_coef: bfloat16 [16384, 512], P('wide'), may hold values from -0.3125 to 0.3125
- vir_coef: bfloat16 [16384, 1024], P('narrow'), may hold values from -0.3125 to 0.3125
Outputs:
- response: float32 [3, 512, 1024], P(None, 'wide', 'narrow')
The draws below stay inside these ranges and needn't reach their ends.
Inputs may be any that keep to these rules, and one draw needn't show every extreme that they name: `tile_dest`: among the routes of one device's 16 tiles, no wide index is named more than 8 times, and some device names some index exactly 8 times; the 2 indices of one tile differ. `point_count`: the counts of all batches sum to 12800.
All inputs are finite; a program needn't handle non-finite values. No bound on the sum of `point_count` on one device may be relied on, other than what follows from the above.
Results may differ from the reference program's by a relative error of at most 0.0074.
Values may be sent and summed in bfloat16 or wider, within the bound.
No kernel may reach another device: no remote copies, remote signals or barrier semaphores. Data moves between devices by JAX's collectives and lax.ppermute only.
A program may use at most 128 MiB of HBM per device.

```python
import math
import jax
import jax.numpy as jnp
import numpy as np
from jax import lax

NAO = 16384
NOCC = 512
NVIR = 1024
BLK = 128
KB = 5
FIELDS = 3
TOP = 2
TILE_DEV = 16
NBAT = 2
PTS = 1280
RB = 16
CB = 32
CAP = 8
TILES = 512
BATCHES = 16
N_WIDE = 8
N_NARROW = 4
DEVICES = 32


def place_ends(drawn, stream_key, least, high):
    index_at = [jax.random.randint(jax.random.fold_in(stream_key, axis), (), 0, length) for axis, length in enumerate(drawn.shape)]
    longest = drawn.shape.index(max(drawn.shape))
    beside = index_at[:longest] + [(index_at[longest] + 1) % drawn.shape[longest]] + index_at[longest + 1:]
    return drawn.at[tuple(index_at)].set(least).at[tuple(beside)].set(high)


def shard_levels(stream_key, dims, cuts, low, largest):
    level, own = 1.0, jax.random.fold_in(stream_key, 6)
    for position, shards_of in cuts:
        heights = jnp.exp(jax.random.uniform(jax.random.fold_in(own, position), (shards_of,), jnp.float32, low / len(cuts), largest / len(cuts)))
        level = level * jnp.repeat(heights, dims[position] // shards_of).reshape([-1 if axis == position else 1 for axis in range(len(dims))])
    return level


def profile(amount, total, reach, lean):
    weights = [(1 << 20) // math.isqrt(standing ** lean) + 1 for standing in range(2, amount + 1)]
    spare, counts = total - reach - (amount - 1), [1] * (amount - 1)
    while spare > 0:
        free = [i for i in range(amount - 1) if counts[i] < reach]
        whole, budget = sum([weights[i] for i in free]), spare
        for i in free:
            more = min(reach - counts[i], max(1, budget * weights[i] // whole), spare)
            counts[i] = counts[i] + more
            spare = spare - more
    return np.array([reach] + counts)


def ragged_sizes(own_key, count, total, bound, slope):
    if count == 2:
        one = jax.random.randint(own_key, (), max(1, total - bound), min(bound, total - 1) + 1)
        return jnp.stack([one, total - one])
    lengths = jnp.asarray(profile(count, total, bound, slope), jnp.int32)
    pairs = (count - 1) // 2
    donor, receiver = lengths[1:1 + 2 * pairs:2], lengths[2:2 + 2 * pairs:2]
    slack = jnp.minimum(donor - 1, bound - receiver)
    moved = jax.random.randint(jax.random.fold_in(own_key, 1), (pairs,), 0, 1 << 20) % (slack + 1)
    lengths = lengths.at[1:1 + 2 * pairs:2].set(donor - moved).at[2:2 + 2 * pairs:2].set(receiver + moved)
    return lengths[jax.random.permutation(jax.random.fold_in(own_key, 2), count)]


def routed_block(stream_key, own, number, rows, number_of, top, limit, lean):
    sequence = jax.random.permutation(stream_key, number_of)
    packed, ordinary = portions_of(number_of, rows * top, limit, lean, True), portions_of(number_of, rows * top, limit, lean, False)
    places = jnp.arange(number_of)

    def named(sizes, rotation):
        used = int((sizes > 0).sum())
        fixed = max(1, used // 4)
        moved = fixed + (places - fixed + rotation * (used - fixed)) % max(1, number_of - fixed)
        return jnp.zeros((number_of,), jnp.int32).at[sequence[jnp.where(places < fixed, places, moved)]].set(jnp.asarray(sizes, jnp.int32))

    sizes = jnp.where(number % 4 == 0, named(packed, number // 4), named(ordinary, number - number // 4 - 1))
    mixed = jax.random.permutation(jax.random.fold_in(own, 3), number_of)
    donor, receiver = mixed[0:number_of // 2 * 2:2], mixed[1:number_of // 2 * 2:2]
    slack = jnp.minimum(sizes[donor] - 1, limit - sizes[receiver]) // 2
    slack = jnp.where((donor == sequence[0]) | (receiver == sequence[0]) | (sizes[receiver] == 0), 0, jnp.maximum(slack, 0))
    moved = jax.random.randint(jax.random.fold_in(own, 4), (number_of // 2,), 0, 1 << 20) % (slack + 1)
    sizes = sizes.at[donor].add(-moved).at[receiver].add(moved)
    labels = jnp.searchsorted(jnp.cumsum(sizes), jnp.arange(rows * top), side="right").astype(jnp.int32)
    listing = labels.reshape(top, rows).T
    listing = listing[jax.random.permutation(jax.random.fold_in(own, 1), rows)]
    rotation = jax.random.randint(jax.random.fold_in(own, 2), (rows, 1), 0, top)
    return jnp.take_along_axis(listing, (jnp.arange(top)[None, :] + rotation) % top, axis=1)


def portions_of(amount, total, reach, skew, full):
    weights = [(1 << 20) // math.isqrt(rank ** skew) + 1 for rank in range(1, amount + 1)]
    largest = reach if full else min(reach, max(-(-total // amount), total * weights[0] // sum(weights)))
    least = 1 if total - largest >= amount - 1 else 0
    counts, spare = [largest] + [least] * (amount - 1), total - largest - least * (amount - 1)
    while spare > 0:
        free = [i for i in range(1, amount) if counts[i] < largest] or [i for i in range(1, amount) if counts[i] < reach]
        mass, left = sum([weights[i] for i in free]), spare
        for i in free:
            addition = min(reach - counts[i], max(1, left * weights[i] // mass), spare)
            counts[i] = counts[i] + addition
            spare = spare - addition
    return np.array(counts)


def scatter_about(key, shape, scale, reach, cuts=(), kind=jnp.bfloat16):
    entries = scale * jax.random.normal(key, shape, jnp.float32)
    if cuts:
        entries = entries * shard_levels(key, shape, cuts, -0.22, 0.18)
    return jnp.clip(entries, -reach, reach).astype(kind)


def setup_inputs(seed: int = 0) -> dict:
    key_list = jax.random.split(jax.random.key(seed), 13)
    dens_tiles = scatter_about(key_list[0], (TILES, FIELDS, BLK, BLK), 1.0, 6.0, ((0, 32),))
    tile_dest_keys = jax.random.split(jax.random.fold_in(key_list[1], 1), TILES // TILE_DEV)
    tile_dest_turns = jax.random.permutation(jax.random.fold_in(key_list[1], 3), TILES // TILE_DEV)
    tile_dest = jax.vmap(lambda own, number: routed_block(jax.random.fold_in(key_list[1], 2), own, number, TILE_DEV, N_WIDE, TOP, CAP, 2))(tile_dest_keys, tile_dest_turns).reshape((TILES, TOP))
    tile_place = place_ends(jax.random.randint(key_list[2], (TILES, TOP), 0, NBAT * KB * KB), jax.random.fold_in(key_list[2], 1), 0, (NBAT * KB * KB) - 1).astype(jnp.int32)
    tile_rows = place_ends(jax.random.randint(key_list[3], (TILES,), 0, RB), jax.random.fold_in(key_list[3], 1), 0, RB - 1).astype(jnp.int32)
    tile_cols = place_ends(jax.random.randint(key_list[4], (TILES,), 0, CB), jax.random.fold_in(key_list[4], 1), 0, CB - 1).astype(jnp.int32)
    ao_values = scatter_about(key_list[5], (BATCHES, KB * BLK, PTS), (KB * BLK) ** -0.5, 0.25, ((0, 8),))
    point_count = ragged_sizes(key_list[6], BATCHES, BATCHES * PTS * 5 // 8, PTS, 2).astype(jnp.int32)
    weights = jnp.clip(jnp.exp(math.log(1.0) - 2.9957323 * jax.random.uniform(key_list[7], (BATCHES, PTS), jnp.float32) ** shard_levels(key_list[7], (BATCHES, PTS), ((0, 8),), -0.2, 0.2)), 0.05, 1.0)
    kernel_first = jnp.clip(-1.5 + 1.2 * jax.random.uniform(key_list[8], (BATCHES, PTS), jnp.float32) ** shard_levels(key_list[8], (BATCHES, PTS), ((0, 8),), -0.2, 0.2), -1.5, -0.3)
    kernel_second = jnp.clip(0.2 + 1.8 * jax.random.uniform(key_list[9], (BATCHES, PTS), jnp.float32) ** shard_levels(key_list[9], (BATCHES, PTS), ((0, 8),), -0.2, 0.2), 0.2, 2.0)
    occ_coef = scatter_about(key_list[10], (NAO, NOCC), (3 * BLK) ** -0.5, 0.3125, ((0, 8),))
    vir_coef = scatter_about(key_list[11], (NAO, NVIR), (3 * BLK) ** -0.5, 0.3125, ((0, 4),))
    return dict(dens_tiles=dens_tiles, tile_dest=tile_dest, tile_place=tile_place, tile_rows=tile_rows, tile_cols=tile_cols, ao_values=ao_values, point_count=point_count, weights=weights, kernel_first=kernel_first, kernel_second=kernel_second, occ_coef=occ_coef, vir_coef=vir_coef)


def field_potential(density, kernel_one, kernel_two, point_scale):
    dens_a = density[:, 0]
    dens_b = density[:, 1]
    dens_c = density[:, 2]
    stacked = jnp.stack([kernel_one * dens_a + kernel_two * dens_b * dens_c,
                         kernel_one * dens_b + kernel_two * dens_a * dens_c,
                         kernel_one * dens_c + kernel_two * dens_a * dens_b], axis=1)
    return stacked * point_scale[:, None, :]


def reference(dens_tiles, tile_dest, tile_place, tile_rows, tile_cols, ao_values, point_count, weights, kernel_first, kernel_second, occ_coef, vir_coef):
    batch_slots = NBAT * KB * KB
    tile_len = FIELDS * BLK * BLK
    ao_width = KB * BLK
    flat_tiles = dens_tiles.reshape(TILES, tile_len).astype(jnp.float32)
    narrow_of = ((jnp.arange(TILES) // TILE_DEV) % N_NARROW).astype(jnp.int32)
    trash = N_NARROW * batch_slots
    ao_all = ao_values.reshape(N_WIDE, NBAT, ao_width, PTS)
    inside = jnp.arange(PTS)[None, :] < point_count[:, None]
    scale_all = jnp.where(inside, weights, jnp.float32(0.0)).reshape(N_WIDE, NBAT, PTS)
    first_all = kernel_first.reshape(N_WIDE, NBAT, PTS)
    second_all = kernel_second.reshape(N_WIDE, NBAT, PTS)

    def receive(wide_idx):
        land_grid = jnp.zeros((trash + 1, tile_len), jnp.float32)
        for route in range(TOP):
            seg_ids = jnp.where(tile_dest[:, route] == wide_idx, narrow_of * batch_slots + tile_place[:, route], trash).astype(jnp.int32)
            land_grid = land_grid + jax.ops.segment_sum(flat_tiles, seg_ids, num_segments=trash + 1)
        land_grid = land_grid[:trash].astype(jnp.bfloat16)
        dens_grid = land_grid.reshape(N_NARROW, NBAT, KB, KB, FIELDS, BLK, BLK).transpose(0, 1, 4, 2, 5, 3, 6)
        dens_grid = dens_grid.reshape(N_NARROW, NBAT, FIELDS, ao_width, ao_width)
        ao_float = lax.dynamic_index_in_dim(ao_all, wide_idx, 0, keepdims=False).astype(jnp.float32)
        mixed_rows = jnp.einsum('cbfmn,bnp->cbfmp', dens_grid.astype(jnp.float32), ao_float)
        density = jnp.sum(jnp.sum(mixed_rows * ao_float[None, :, None], axis=3), axis=0)
        point_scale = lax.dynamic_index_in_dim(scale_all, wide_idx, 0, keepdims=False)
        kernel_one = lax.dynamic_index_in_dim(first_all, wide_idx, 0, keepdims=False)
        kernel_two = lax.dynamic_index_in_dim(second_all, wide_idx, 0, keepdims=False)
        potential = field_potential(density, kernel_one, kernel_two, point_scale)
        scaled = (ao_float[:, None] * potential[:, :, None, :]).astype(jnp.bfloat16)
        blocks = jnp.einsum('bfmp,bnp->bfmn', scaled.astype(jnp.float32), ao_float)
        blocks = blocks.reshape(NBAT, FIELDS, KB, BLK, KB, BLK).transpose(0, 2, 4, 1, 3, 5)
        return blocks.reshape(batch_slots, tile_len).astype(jnp.bfloat16)

    answers = lax.map(receive, jnp.arange(N_WIDE, dtype=jnp.int32))
    tile_potential = jnp.zeros((TILES, tile_len), jnp.float32)
    for route in range(TOP):
        tile_potential = tile_potential + answers[tile_dest[:, route], tile_place[:, route]].astype(jnp.float32)
    tile_potential = tile_potential.astype(jnp.bfloat16).reshape(DEVICES, TILE_DEV, FIELDS, BLK, BLK)
    occ_blocks = occ_coef.reshape(NAO // BLK, BLK, NOCC)
    vir_blocks = vir_coef.reshape(NAO // BLK, BLK, NVIR)
    rows_dev = tile_rows.reshape(DEVICES, TILE_DEV)
    cols_dev = tile_cols.reshape(DEVICES, TILE_DEV)

    def project(summed, carried):
        device, pieces, occ_rows, vir_cols = carried
        wide_idx = device // N_NARROW
        narrow_idx = device % N_NARROW
        occ_sel = occ_blocks[wide_idx * RB + occ_rows].astype(jnp.float32)
        vir_sel = vir_blocks[narrow_idx * CB + vir_cols].reshape(TILE_DEV * BLK, NVIR)
        left_half = jnp.einsum('tao,tfab->fotb', occ_sel, pieces.astype(jnp.float32)).astype(jnp.bfloat16)
        term = jnp.dot(left_half.reshape(FIELDS * NOCC, TILE_DEV * BLK), vir_sel, preferred_element_type=jnp.float32)
        return summed + term.reshape(FIELDS, NOCC, NVIR), None

    start = jnp.zeros((FIELDS, NOCC, NVIR), jnp.float32)
    response, _ = lax.scan(project, start, (jnp.arange(DEVICES, dtype=jnp.int32), tile_potential, rows_dev, cols_dev))
    return response
```

```python
import functools

import jax
import jax.numpy as jnp
from jax import lax
from jax.experimental import pallas as pl
from jax.experimental.pallas import tpu as pltpu
from jax.sharding import PartitionSpec as P

BLK = 128
KB = 5
FIELDS = 3
TOP = 2
NBAT = 2
ANY = pl.BlockSpec(memory_space=pl.ANY)
VMEM = pl.BlockSpec(memory_space=pltpu.VMEM)
SMEM = pl.BlockSpec(memory_space=pltpu.SMEM)
VMEM_LIMIT = 60 * 1024 * 1024


def density_kernel(count, groups, slot_ref, dest_ref, row_ref, col_ref, *refs):
    ao_refs = refs[:count]
    tile_refs = refs[count : count + groups]
    out_ref, held, sems = refs[count + groups :]
    copies = [pltpu.make_async_copy(ao_refs[i], held.at[i], sems.at[i]) for i in range(count)]
    for copy in copies:
        copy.start()
    out_ref[...] = jnp.zeros_like(out_ref)
    for copy in copies:
        copy.wait()
    tiles = tile_refs[0].shape[0]
    points = held.shape[2]
    for group in range(groups):
        tile_ref = tile_refs[group]

        def step(i, carry, group=group, tile_ref=tile_ref):
            at = group * tiles * TOP + i
            slot = slot_ref[at]

            @pl.when(slot >= 0)
            def _():
                left = tile_ref[i // TOP]
                rows = pl.ds(pl.multiple_of(row_ref[at] * BLK, BLK), BLK)
                cols = pl.ds(pl.multiple_of(col_ref[at] * BLK, BLK), BLK)
                dest = dest_ref[at]
                for low in range(0, points, 256):
                    lanes = slice(low, min(low + 256, points))
                    mixed = jnp.dot(left, held[slot, cols, lanes], preferred_element_type=jnp.float32)
                    mixed = mixed.reshape(FIELDS, BLK, mixed.shape[-1])
                    value = held[slot, rows, lanes].astype(jnp.float32)
                    out_ref[dest, :, lanes] += jnp.sum(mixed * value[None], axis=1)

            return carry

        lax.fori_loop(0, tiles * TOP, step, 0)


def density_call(slots, dests, rows, cols, ao_list, tile_list, wide_count):
    count, groups = len(ao_list), len(tile_list)
    height, points = ao_list[0].shape
    return pl.pallas_call(
        functools.partial(density_kernel, count, groups),
        out_shape=jax.ShapeDtypeStruct((wide_count, FIELDS, points), jnp.float32),
        in_specs=[SMEM] * 4 + [ANY] * count + [VMEM] * groups,
        out_specs=VMEM,
        scratch_shapes=[
            pltpu.VMEM((count, height, points), jnp.bfloat16),
            pltpu.SemaphoreType.DMA((count,)),
        ],
        compiler_params=pltpu.CompilerParams(vmem_limit_bytes=24 * 1024 * 1024),
        cost_estimate=pl.CostEstimate(
            flops=1_000_000_000, bytes_accessed=10_000_000, transcendentals=0
        ),
        name="density",
    )(slots, dests, rows, cols, *ao_list, *tile_list)


def block_kernel(count, groups, place_ref, slot_ref, row_ref, col_ref, pot_ref, *refs):
    ao_refs = refs[:count]
    out_refs = refs[count : count + groups]
    held, total, sems = refs[count + groups :]

    def each(act):
        for i in range(count):

            @pl.when(place_ref[i] >= 0)
            def _():
                act(pltpu.make_async_copy(ao_refs[i], held.at[place_ref[i]], sems.at[i]))

    each(lambda copy: copy.start())
    each(lambda copy: copy.wait())
    tiles = out_refs[0].shape[0]
    for group in range(groups):
        out_ref = out_refs[group]

        def step(t, carry, group=group, out_ref=out_ref):
            total[...] = jnp.zeros_like(total)
            for k in range(TOP):
                at = (group * tiles + t) * TOP + k
                slot = slot_ref[at]

                @pl.when(slot >= 0)
                def _():
                    rows = pl.ds(pl.multiple_of(row_ref[at] * BLK, BLK), BLK)
                    cols = pl.ds(pl.multiple_of(col_ref[at] * BLK, BLK), BLK)
                    value = held[slot, rows, :].astype(jnp.float32)
                    right = held[slot, cols, :]
                    for f in range(FIELDS):
                        scaled = (value * pot_ref[slot, f : f + 1, :]).astype(jnp.bfloat16)
                        total[f] += lax.dot_general(
                            scaled,
                            right,
                            (((1,), (1,)), ((), ())),
                            preferred_element_type=jnp.float32,
                        )

            out_ref[t] = total[...].astype(jnp.bfloat16)
            return carry

        lax.fori_loop(0, tiles, step, 0)


def block_call(places, slots, rows, cols, potential, ao_list, groups, tiles):
    count = len(ao_list)
    height, points = ao_list[0].shape
    wide_count = potential.shape[0]
    return pl.pallas_call(
        functools.partial(block_kernel, count, groups),
        out_shape=[jax.ShapeDtypeStruct((tiles, FIELDS, BLK, BLK), jnp.bfloat16)] * groups,
        in_specs=[SMEM] * 4 + [VMEM] + [ANY] * count,
        out_specs=[VMEM] * groups,
        scratch_shapes=[
            pltpu.VMEM((wide_count, height, points), jnp.bfloat16),
            pltpu.VMEM((FIELDS, BLK, BLK), jnp.float32),
            pltpu.SemaphoreType.DMA((count,)),
        ],
        compiler_params=pltpu.CompilerParams(vmem_limit_bytes=VMEM_LIMIT),
        cost_estimate=pl.CostEstimate(
            flops=4_000_000_000, bytes_accessed=20_000_000, transcendentals=0
        ),
        name="blocks",
    )(places, slots, rows, cols, potential, *ao_list)


def body(
    dens_tiles,
    tile_dest,
    tile_place,
    tile_rows,
    tile_cols,
    ao_values,
    point_count,
    weights,
    kernel_first,
    kernel_second,
    occ_coef,
    vir_coef,
):
    wide_count = lax.axis_size("wide")
    narrow_count = lax.axis_size("narrow")
    tile_count = dens_tiles.shape[0]
    nocc, nvir = occ_coef.shape[1], vir_coef.shape[1]
    halves = narrow_count // NBAT
    points = ao_values.shape[2] // halves
    line = wide_count // 2
    wide = lax.axis_index("wide")
    narrow = lax.axis_index("narrow")
    batch, half = narrow // halves, narrow % halves
    level = wide // 2

    def across(x, least=0, most=line - 1):
        pairs = [(i, i ^ 1) for i in range(wide_count) if least <= i // 2 <= most]
        return lax.ppermute(x, "wide", pairs)

    def upward(x, k):
        return lax.ppermute(
            x, "wide", [(i, i + 2) for i in range(wide_count - 2) if i // 2 >= k - 1]
        )

    def downward(x, k):
        return lax.ppermute(
            x, "wide", [(i, i - 2) for i in range(2, wide_count) if i // 2 <= line - k]
        )

    def beside(x, mask):
        return lax.ppermute(x, "narrow", [(i, i ^ mask) for i in range(narrow_count)])

    own = lax.dynamic_slice(
        ao_values, (batch, 0, half * points), (1, ao_values.shape[1], points)
    )[0]
    up, down = {0: own}, {0: own}
    ao_stages = [[own, across(own)]]
    ao_places = [wide, wide ^ 1]
    tiles = dens_tiles.reshape(tile_count, FIELDS * BLK, BLK)
    for k in range(1, line):
        up[k] = upward(up[k - 1], k)
        down[k] = downward(down[k - 1], k)
        up_beside = across(up[k], least=k)
        down_beside = across(down[k], most=line - 1 - k)
        ao_stages.append([up[k], up_beside, down[k], down_beside])
        low_ok, high_ok = level >= k, level + k < line
        ao_places += [
            jnp.where(low_ok, wide - 2 * k, -1),
            jnp.where(low_ok, (wide - 2 * k) ^ 1, -1),
            jnp.where(high_ok, wide + 2 * k, -1),
            jnp.where(high_ok, (wide + 2 * k) ^ 1, -1),
        ]
    tile_list = [tiles]
    mask = 1
    while mask < narrow_count:
        tile_list += [beside(x, mask) for x in tile_list]
        mask *= 2

    routes = jnp.stack([tile_dest, tile_place]).reshape(1, -1)
    routes = lax.all_to_all(
        jnp.broadcast_to(routes, (narrow_count, routes.shape[1])),
        "narrow",
        split_axis=0,
        concat_axis=0,
        tiled=True,
    )
    routes = jnp.take(routes, narrow ^ jnp.arange(narrow_count), axis=0)
    routes = routes.reshape(narrow_count, 2, tile_count * TOP)
    dests, places = routes[:, 0].reshape(-1), routes[:, 1].reshape(-1)
    mine = places // (KB * KB) == batch
    rows = places % (KB * KB) // KB
    cols = places % KB
    offset = dests // 2 - level
    other = (dests ^ wide) & 1
    density = None
    for k in range(line):
        index = other + 2 * (offset > 0).astype(jnp.int32) if k else other
        slots = jnp.where(mine & (jnp.abs(offset) == k), index, -1)
        part = density_call(slots, dests, rows, cols, ao_stages[k], tile_list, wide_count)
        density = part if density is None else density + part
    density = lax.all_to_all(density, "wide", split_axis=0, concat_axis=0, tiled=True)
    density = jnp.sum(density, axis=0)

    def here(x):
        return lax.dynamic_slice(x, (batch, half * points), (1, points))

    used = lax.dynamic_slice(point_count, (batch,), (1,))
    inside = (half * points + jnp.arange(points))[None, :] < used[:, None]
    scale = jnp.where(inside, here(weights), jnp.float32(0.0))
    first, second = here(kernel_first), here(kernel_second)
    product = jnp.stack([density[1] * density[2], density[0] * density[2], density[0] * density[1]])
    potential = (first * density + second * product) * scale
    potential = lax.all_to_all(
        jnp.broadcast_to(potential[None], (wide_count,) + potential.shape),
        "wide",
        split_axis=0,
        concat_axis=0,
        tiled=True,
    )
    blocks = block_call(
        jnp.stack(ao_places),
        jnp.where(mine, dests, -1),
        rows,
        cols,
        potential,
        [x for stage in ao_stages for x in stage],
        narrow_count,
        tile_count,
    )
    sums = list(blocks)
    mask = 1
    while len(sums) > 1:
        sums = [
            (
                sums[i].astype(jnp.float32) + beside(sums[i + 1], mask).astype(jnp.float32)
            ).astype(jnp.bfloat16)
            for i in range(0, len(sums), 2)
        ]
        mask *= 2
    tile_potential = sums[0]

    occ_sel = occ_coef.reshape(-1, BLK, nocc)[tile_rows]
    vir_sel = vir_coef.reshape(-1, BLK, nvir)[tile_cols].reshape(tile_count * BLK, nvir)
    left_half = jnp.einsum(
        "tao,tfab->fotb", occ_sel, tile_potential, preferred_element_type=jnp.float32
    ).astype(jnp.bfloat16)
    partial_value = jnp.dot(
        left_half.reshape(FIELDS * nocc, tile_count * BLK),
        vir_sel,
        preferred_element_type=jnp.float32,
    ).astype(jnp.bfloat16)
    columns = partial_value.reshape(FIELDS * nocc, narrow_count, nvir // narrow_count)
    columns = lax.all_to_all(
        columns.transpose(1, 0, 2), "narrow", split_axis=0, concat_axis=0, tiled=True
    )
    columns = jnp.sum(columns.astype(jnp.float32), axis=0).astype(jnp.bfloat16)
    pieces = columns.reshape(FIELDS, wide_count, nocc // wide_count, nvir // narrow_count)
    pieces = lax.all_to_all(
        pieces.transpose(1, 0, 2, 3), "wide", split_axis=0, concat_axis=0, tiled=True
    )
    return jnp.sum(pieces.astype(jnp.float32), axis=0)


def solution(mesh):
    in_specs = (
        P(("wide", "narrow"), None, None, None),
        P(("wide", "narrow"), None),
        P(("wide", "narrow"), None),
        P(("wide", "narrow")),
        P(("wide", "narrow")),
        P("wide", None, None),
        P("wide"),
        P("wide", None),
        P("wide", None),
        P("wide", None),
        P("wide", None),
        P("narrow", None),
    )
    out_specs = P(None, "wide", "narrow")
    return jax.shard_map(body, mesh=mesh, in_specs=in_specs, out_specs=out_specs, check_vma=False)
```

```python
import functools

import jax
import jax.numpy as jnp
from jax import lax
from jax.experimental import pallas as pl
from jax.experimental.pallas import tpu as pltpu
from jax.sharding import PartitionSpec as P


BLK = 128
KB = 5
FIELDS = 3
TOP = 2
NBAT = 2
ANY = pl.BlockSpec(memory_space=pl.ANY)
VMEM = pl.BlockSpec(memory_space=pltpu.VMEM)
SMEM = pl.BlockSpec(memory_space=pltpu.SMEM)


def density_kernel(count, groups, slot_ref, dest_ref, row_ref, col_ref, *refs):
    ao_refs = refs[:count]
    tile_refs = refs[count : count + groups]
    out_ref, held, sems = refs[count + groups :]
    copies = [pltpu.make_async_copy(ao_refs[i], held.at[i], sems.at[i]) for i in range(count)]
    for copy in copies:
        copy.start()
    out_ref[...] = jnp.zeros_like(out_ref)
    for copy in copies:
        copy.wait()
    tiles = tile_refs[0].shape[0]
    points = held.shape[2]
    for group in range(groups):
        tile_ref = tile_refs[group]

        def step(i, carry, group=group, tile_ref=tile_ref):
            at = group * tiles * TOP + i
            slot = slot_ref[at]

            @pl.when(slot >= 0)
            def _():
                left = tile_ref[i // TOP]
                rows = pl.ds(pl.multiple_of(row_ref[at] * BLK, BLK), BLK)
                cols = pl.ds(pl.multiple_of(col_ref[at] * BLK, BLK), BLK)
                dest = dest_ref[at]
                for low in range(0, points, 256):
                    lanes = slice(low, min(low + 256, points))
                    mixed = jnp.dot(left, held[slot, cols, lanes], preferred_element_type=jnp.float32)
                    mixed = mixed.reshape(FIELDS, BLK, mixed.shape[-1])
                    value = held[slot, rows, lanes].astype(jnp.float32)
                    out_ref[dest, :, lanes] += jnp.sum(mixed * value[None], axis=1)

            return carry

        lax.fori_loop(0, tiles * TOP, step, 0)


def density_call(slots, dests, rows, cols, ao_list, tile_list, wide_count):
    count, groups = len(ao_list), len(tile_list)
    height, points = ao_list[0].shape
    return pl.pallas_call(
        functools.partial(density_kernel, count, groups),
        out_shape=jax.ShapeDtypeStruct((wide_count, FIELDS, points), jnp.float32),
        in_specs=[SMEM] * 4 + [ANY] * count + [VMEM] * groups,
        out_specs=VMEM,
        scratch_shapes=[
            pltpu.VMEM((count, height, points), jnp.bfloat16),
            pltpu.SemaphoreType.DMA((count,)),
        ],
        compiler_params=pltpu.CompilerParams(vmem_limit_bytes=24 * 1024 * 1024),
        cost_estimate=pl.CostEstimate(
            flops=1_000_000_000, bytes_accessed=10_000_000, transcendentals=0
        ),
        name="density",
    )(slots, dests, rows, cols, *ao_list, *tile_list)


def block_kernel(count, groups, first, place_ref, slot_ref, row_ref, col_ref, pot_ref, *refs):
    ao_refs = refs[:count]
    out_refs = refs[count : count + groups * FIELDS]
    held, total, sems = refs[count + groups * FIELDS :]

    def each(act):
        for i in range(count):

            @pl.when(place_ref[i] >= 0)
            def _():
                act(pltpu.make_async_copy(ao_refs[i], held.at[place_ref[i]], sems.at[i]))

    each(lambda copy: copy.start())
    each(lambda copy: copy.wait())
    tiles = out_refs[0].shape[0]
    for group in range(groups):

        def step(t, carry, group=group):
            total[...] = jnp.zeros_like(total)
            for k in range(TOP):
                at = ((first + group) * tiles + t) * TOP + k
                slot = slot_ref[at]

                @pl.when(slot >= 0)
                def _():
                    rows = pl.ds(pl.multiple_of(row_ref[at] * BLK, BLK), BLK)
                    cols = pl.ds(pl.multiple_of(col_ref[at] * BLK, BLK), BLK)
                    value = held[slot, rows, :].astype(jnp.float32)
                    right = held[slot, cols, :]
                    for f in range(FIELDS):
                        scaled = (value * pot_ref[slot, f : f + 1, :]).astype(jnp.bfloat16)
                        total[f] += lax.dot_general(
                            scaled,
                            right,
                            (((1,), (1,)), ((), ())),
                            preferred_element_type=jnp.float32,
                        )

            for f in range(FIELDS):
                out_refs[group * FIELDS + f][t] = total[f].astype(jnp.bfloat16)
            return carry

        lax.fori_loop(0, tiles, step, 0)


def block_call(first, groups, places, slots, rows, cols, potential, ao_list, tiles):
    count = len(ao_list)
    height, points = ao_list[0].shape
    wide_count = potential.shape[0]
    outs = pl.pallas_call(
        functools.partial(block_kernel, count, groups, first),
        out_shape=[jax.ShapeDtypeStruct((tiles, BLK, BLK), jnp.bfloat16)] * (groups * FIELDS),
        in_specs=[SMEM] * 4 + [VMEM] + [ANY] * count,
        out_specs=[VMEM] * (groups * FIELDS),
        scratch_shapes=[
            pltpu.VMEM((wide_count, height, points), jnp.bfloat16),
            pltpu.VMEM((FIELDS, BLK, BLK), jnp.float32),
            pltpu.SemaphoreType.DMA((count,)),
        ],
        compiler_params=pltpu.CompilerParams(vmem_limit_bytes=40 * 1024 * 1024),
        cost_estimate=pl.CostEstimate(
            flops=2_000_000_000 * groups, bytes_accessed=10_000_000, transcendentals=0
        ),
        name="blocks",
    )(places, slots, rows, cols, potential, *ao_list)
    return [outs[g * FIELDS : (g + 1) * FIELDS] for g in range(groups)]


def project_kernel(parts, where_ref, *refs):
    part_refs = refs[:parts]
    occ_ref, vir_ref, even_ref, odd_ref, left_ref = refs[parts:]
    wide_at, narrow_at, wide_count = where_ref[0], where_ref[1], where_ref.shape[0] - 2
    tiles, nocc = occ_ref.shape[:2]
    owned = nocc // wide_count
    pieces = even_ref.shape[0] + odd_ref.shape[0]
    width = vir_ref.shape[1] // pieces

    def fill(t, carry):
        block = part_refs[0][t].astype(jnp.float32)
        for ref in part_refs[1:]:
            block += ref[t].astype(jnp.float32)
        left = jnp.dot(
            occ_ref[t], block.astype(jnp.bfloat16), preferred_element_type=jnp.float32
        ).astype(jnp.bfloat16)
        lanes = pl.ds(pl.multiple_of(t * BLK, BLK), BLK)
        for q in range(wide_count):
            at = pl.multiple_of((wide_at ^ q) * owned, owned)
            left_ref[pl.ds(at, owned), lanes] = left[q * owned : (q + 1) * owned]
        return carry

    lax.fori_loop(0, tiles, fill, 0)
    for j in range(pieces):
        lanes = pl.ds(pl.multiple_of((narrow_at ^ j) * width, width), width)
        value = jnp.dot(left_ref[...], vir_ref[:, lanes], preferred_element_type=jnp.float32)
        if j % 2:
            odd_ref[j // 2] = value.astype(jnp.bfloat16)
        else:
            even_ref[j // 2] = value


def project_call(where, part_list, occ_sel, vir_sel, narrow_count):
    _, nocc = occ_sel.shape[:2]
    depth, nvir = vir_sel.shape
    shape = (narrow_count // 2, nocc, nvir // narrow_count)
    return pl.pallas_call(
        functools.partial(project_kernel, len(part_list)),
        out_shape=[
            jax.ShapeDtypeStruct(shape, jnp.float32),
            jax.ShapeDtypeStruct(shape, jnp.bfloat16),
        ],
        in_specs=[SMEM] + [VMEM] * (len(part_list) + 2),
        out_specs=[VMEM] * 2,
        scratch_shapes=[pltpu.VMEM((nocc, depth), jnp.bfloat16)],
        compiler_params=pltpu.CompilerParams(vmem_limit_bytes=32 * 1024 * 1024),
        cost_estimate=pl.CostEstimate(
            flops=2_400_000_000, bytes_accessed=10_000_000, transcendentals=0
        ),
        name="project",
    )(where, *part_list, occ_sel, vir_sel)


def body(
    dens_tiles,
    tile_dest,
    tile_place,
    tile_rows,
    tile_cols,
    ao_values,
    point_count,
    weights,
    kernel_first,
    kernel_second,
    occ_coef,
    vir_coef,
):
    wide_count = lax.axis_size("wide")
    narrow_count = lax.axis_size("narrow")
    tile_count = dens_tiles.shape[0]
    nocc, nvir = occ_coef.shape[1], vir_coef.shape[1]
    halves = narrow_count // NBAT
    points = ao_values.shape[2] // halves
    line = wide_count // 2
    wide = lax.axis_index("wide")
    narrow = lax.axis_index("narrow")
    batch, half = narrow // halves, narrow % halves
    level = wide // 2

    def across(x, least=0, most=line - 1):
        pairs = [(i, i ^ 1) for i in range(wide_count) if least <= i // 2 <= most]
        return lax.ppermute(x, "wide", pairs)

    def upward(x, k):
        return lax.ppermute(
            x, "wide", [(i, i + 2) for i in range(wide_count - 2) if i // 2 >= k - 1]
        )

    def downward(x, k):
        return lax.ppermute(
            x, "wide", [(i, i - 2) for i in range(2, wide_count) if i // 2 <= line - k]
        )

    def beside(x, mask):
        return lax.ppermute(x, "narrow", [(i, i ^ mask) for i in range(narrow_count)])

    own = lax.dynamic_slice(
        ao_values, (batch, 0, half * points), (1, ao_values.shape[1], points)
    )[0]
    up, down = {0: own}, {0: own}
    own_beside = across(own)
    ao_stages = [[own, own_beside]]
    ao_places = [wide, wide ^ 1]
    tiles = dens_tiles.reshape(tile_count, FIELDS * BLK, BLK)
    for k in range(1, line):
        up[k] = upward(up[k - 1], k)
        down[k] = downward(down[k - 1], k)
        up_beside = across(up[k], least=k)
        down_beside = across(down[k], most=line - 1 - k)
        ao_stages.append([up[k], up_beside, down[k], down_beside])
        low_ok, high_ok = level >= k, level + k < line
        ao_places += [
            jnp.where(low_ok, wide - 2 * k, -1),
            jnp.where(low_ok, (wide - 2 * k) ^ 1, -1),
            jnp.where(high_ok, wide + 2 * k, -1),
            jnp.where(high_ok, (wide + 2 * k) ^ 1, -1),
        ]
    routes = jnp.stack([tile_dest, tile_place]).reshape(1, -1)
    routes = lax.all_to_all(
        jnp.broadcast_to(routes, (narrow_count, routes.shape[1])),
        "narrow",
        split_axis=0,
        concat_axis=0,
        tiled=True,
    )
    tiles, routes = lax.optimization_barrier((tiles, routes))
    tile_list = [tiles]
    mask = narrow_count // 2
    while mask:
        pairs = []
        for x in tile_list:
            pairs += [x, beside(x, mask)]
        tile_list = pairs
        mask //= 2

    routes = jnp.take(routes, narrow ^ jnp.arange(narrow_count), axis=0)
    routes = routes.reshape(narrow_count, 2, tile_count * TOP)
    dests, places = routes[:, 0].reshape(-1), routes[:, 1].reshape(-1)
    mine = places // (KB * KB) == batch
    rows = places % (KB * KB) // KB
    cols = places % KB
    offset = dests // 2 - level
    other = (dests ^ wide) & 1
    occ_sel = occ_coef.reshape(-1, BLK, nocc)[tile_rows].transpose(0, 2, 1)
    vir_sel = vir_coef.reshape(-1, BLK, nvir)[tile_cols].reshape(tile_count * BLK, nvir)
    dests, occ_sel, vir_sel = lax.optimization_barrier((dests, occ_sel, vir_sel))
    density = None
    for k in range(line):
        index = other + 2 * (offset > 0).astype(jnp.int32) if k else other
        slots = jnp.where(mine & (jnp.abs(offset) == k), index, -1)
        if density is not None:
            slots, density = lax.optimization_barrier((slots, density))
        part = density_call(slots, dests, rows, cols, ao_stages[k], tile_list, wide_count)
        density = part if density is None else density + part
    density = lax.all_to_all(density, "wide", split_axis=0, concat_axis=0, tiled=True)
    density = jnp.sum(density, axis=0)

    def here(x):
        return lax.dynamic_slice(x, (batch, half * points), (1, points))

    used = lax.dynamic_slice(point_count, (batch,), (1,))
    inside = (half * points + jnp.arange(points))[None, :] < used[:, None]
    scale = jnp.where(inside, here(weights), jnp.float32(0.0))
    first, second = here(kernel_first), here(kernel_second)
    product = jnp.stack([density[1] * density[2], density[0] * density[2], density[0] * density[1]])
    potential = (first * density + second * product) * scale
    potential = lax.all_to_all(
        jnp.broadcast_to(potential[None], (wide_count,) + potential.shape),
        "wide",
        split_axis=0,
        concat_axis=0,
        tiled=True,
    )
    ao_list = [x for stage in ao_stages for x in stage]
    held_places = jnp.stack(ao_places)
    kept = jnp.where(mine, dests, -1)
    where = jnp.concatenate([jnp.stack([wide, narrow]), jnp.zeros((wide_count,), jnp.int32)])

    half_count = narrow_count // 2
    far = block_call(
        half_count, half_count, held_places, kept, rows, cols, potential, ao_list, tile_count
    )

    def fold(groups):
        mask = 1
        while len(groups) > 1:
            groups = [
                [
                    (p.astype(jnp.float32) + beside(q, mask).astype(jnp.float32)).astype(
                        jnp.bfloat16
                    )
                    for p, q in zip(groups[i], groups[i + 1])
                ]
                for i in range(0, len(groups), 2)
            ]
            mask *= 2
        return groups[0]

    far_sum = fold(far)
    potential, far_sum = lax.optimization_barrier((potential, far_sum))
    far_parts = []
    for f in range(FIELDS):
        far_parts.append(beside(far_sum[f], half_count))
    far_sum = far_parts
    near = block_call(0, half_count, held_places, kept, rows, cols, potential, ao_list, tile_count)
    near_sum = fold(near)
    results = []
    for f in range(FIELDS):
        even, odd = project_call(where, [near_sum[f], far_sum[f]], occ_sel, vir_sel, narrow_count)
        mask = 1
        while True:
            even = even + beside(odd, mask).astype(jnp.float32)
            mask *= 2
            if mask == narrow_count:
                break
            even = even.reshape((-1, 2) + even.shape[1:])
            even, odd = even[:, 0], even[:, 1].astype(jnp.bfloat16)
        value = even.reshape(wide_count, nocc // wide_count, nvir // narrow_count)
        mask = 1
        while mask < wide_count:
            value = value.reshape((-1, 2) + value.shape[1:])
            sent = lax.ppermute(
                value[:, 1].astype(jnp.bfloat16),
                "wide",
                [(i, i ^ mask) for i in range(wide_count)],
            )
            value = value[:, 0] + sent.astype(jnp.float32)
            mask *= 2
        results.append(value[0])
    return jnp.stack(results)


def solution(mesh):
    in_specs = (
        P(("wide", "narrow"), None, None, None),
        P(("wide", "narrow"), None),
        P(("wide", "narrow"), None),
        P(("wide", "narrow")),
        P(("wide", "narrow")),
        P("wide", None, None),
        P("wide"),
        P("wide", None),
        P("wide", None),
        P("wide", None),
        P("wide", None),
        P("narrow", None),
    )
    out_specs = P(None, "wide", "narrow")

    return jax.shard_map(body, mesh=mesh, in_specs=in_specs, out_specs=out_specs, check_vma=False)
```

```python
import functools

import jax
import jax.numpy as jnp
from jax import lax
from jax.experimental import pallas as pl
from jax.experimental.pallas import tpu as pltpu
from jax.sharding import PartitionSpec as P


BLK = 128
KB = 5
FIELDS = 3
TOP = 2
NBAT = 2
UNROLL = 2
ANY = pl.BlockSpec(memory_space=pl.ANY)
VMEM = pl.BlockSpec(memory_space=pltpu.VMEM)
SMEM = pl.BlockSpec(memory_space=pltpu.SMEM)
VMEM_LIMIT = 60 * 1024 * 1024


def density_kernel(count, order_ref, slot_ref, dest_ref, row_ref, col_ref, *refs):
    ao_refs = refs[:count]
    tile_ref, out_ref, held, total, sems = refs[count:]
    copies = [pltpu.make_async_copy(ao_refs[i], held.at[i], sems.at[i]) for i in range(count)]
    for copy in copies:
        copy.start()
    total[...] = jnp.zeros_like(total)
    for copy in copies:
        copy.wait()
    points = held.shape[2]
    last = tile_ref.shape[0] - 1

    def one(at):
        slot = slot_ref[at]
        left = tile_ref[jnp.minimum(at // TOP, last)]
        rows = pl.ds(pl.multiple_of(row_ref[at] * BLK, BLK), BLK)
        cols = pl.ds(pl.multiple_of(col_ref[at] * BLK, BLK), BLK)
        sums = []
        for low in range(0, points, 256):
            lanes = slice(low, min(low + 256, points))
            mixed = jnp.dot(left, held[slot, cols, lanes], preferred_element_type=jnp.float32)
            width = mixed.shape[-1]
            value = held[slot, rows, lanes].astype(jnp.float32)
            product = mixed.reshape(FIELDS, BLK, width) * value[None]
            sums.append((lanes, jnp.sum(product.reshape(FIELDS, BLK // 8, 8, width), axis=1)))
        return sums

    def step(i, carry):
        found = [order_ref[UNROLL * i + u] for u in range(UNROLL)]
        values = [one(at) for at in found]
        for at, sums in zip(found, values):
            dest = dest_ref[at]
            for lanes, value in sums:
                total[dest, :, :, lanes] += value
        return carry

    steps = (order_ref[order_ref.shape[0] - 1] + UNROLL - 1) // UNROLL
    lax.fori_loop(0, steps, step, 0)
    out_ref[...] = jnp.sum(total[: out_ref.shape[0]], axis=2)


def density_call(order, slots, dests, rows, cols, ao_list, tiles, wide_count):
    count = len(ao_list)
    height, points = ao_list[0].shape
    return pl.pallas_call(
        functools.partial(density_kernel, count),
        out_shape=jax.ShapeDtypeStruct((wide_count, FIELDS, points), jnp.float32),
        in_specs=[SMEM] * 5 + [ANY] * count + [VMEM],
        out_specs=VMEM,
        scratch_shapes=[
            pltpu.VMEM((count, height, points), jnp.bfloat16),
            pltpu.VMEM((wide_count + 1, FIELDS, 8, points), jnp.float32),
            pltpu.SemaphoreType.DMA((count,)),
        ],
        compiler_params=pltpu.CompilerParams(vmem_limit_bytes=24 * 1024 * 1024),
        cost_estimate=pl.CostEstimate(
            flops=1_000_000_000, bytes_accessed=10_000_000, transcendentals=0
        ),
        name="density",
    )(order, slots, dests, rows, cols, *ao_list, tiles)


def block_kernel(count, groups, first, place_ref, slot_ref, row_ref, col_ref, pot_ref, *refs):
    ao_refs = refs[:count]
    out_refs = refs[count : count + groups * FIELDS]
    held, total, sems = refs[count + groups * FIELDS :]

    def each(act):
        for i in range(count):

            @pl.when(place_ref[i] >= 0)
            def _():
                act(pltpu.make_async_copy(ao_refs[i], held.at[place_ref[i]], sems.at[i]))

    each(lambda copy: copy.start())
    each(lambda copy: copy.wait())
    tiles = out_refs[0].shape[0]
    for group in range(groups):

        def step(t, carry, group=group):
            total[...] = jnp.zeros_like(total)
            for k in range(TOP):
                at = ((first + group) * tiles + t) * TOP + k
                slot = slot_ref[at]

                @pl.when(slot >= 0)
                def _():
                    rows = pl.ds(pl.multiple_of(row_ref[at] * BLK, BLK), BLK)
                    cols = pl.ds(pl.multiple_of(col_ref[at] * BLK, BLK), BLK)
                    value = held[slot, rows, :].astype(jnp.float32)
                    right = held[slot, cols, :]
                    for f in range(FIELDS):
                        scaled = (value * pot_ref[slot, f : f + 1, :]).astype(jnp.bfloat16)
                        total[f] += lax.dot_general(
                            scaled,
                            right,
                            (((1,), (1,)), ((), ())),
                            preferred_element_type=jnp.float32,
                        )

            for f in range(FIELDS):
                out_refs[group * FIELDS + f][t] = total[f].astype(jnp.bfloat16)
            return carry

        lax.fori_loop(0, tiles, step, 0)


def block_call(first, groups, places, slots, rows, cols, potential, ao_list, tiles):
    count = len(ao_list)
    height, points = ao_list[0].shape
    wide_count = potential.shape[0]
    outs = pl.pallas_call(
        functools.partial(block_kernel, count, groups, first),
        out_shape=[jax.ShapeDtypeStruct((tiles, BLK, BLK), jnp.bfloat16)] * (groups * FIELDS),
        in_specs=[SMEM] * 4 + [VMEM] + [ANY] * count,
        out_specs=[VMEM] * (groups * FIELDS),
        scratch_shapes=[
            pltpu.VMEM((wide_count, height, points), jnp.bfloat16),
            pltpu.VMEM((FIELDS, BLK, BLK), jnp.float32),
            pltpu.SemaphoreType.DMA((count,)),
        ],
        compiler_params=pltpu.CompilerParams(vmem_limit_bytes=VMEM_LIMIT),
        cost_estimate=pl.CostEstimate(
            flops=2_000_000_000 * groups, bytes_accessed=10_000_000, transcendentals=0
        ),
        name="blocks",
    )(places, slots, rows, cols, potential, *ao_list)
    return [outs[g * FIELDS : (g + 1) * FIELDS] for g in range(groups)]


def project_kernel(parts, where_ref, *refs):
    part_refs = refs[:parts]
    occ_ref, vir_ref, even_ref, odd_ref, left_ref = refs[parts:]
    wide_at, narrow_at, wide_count = where_ref[0], where_ref[1], where_ref.shape[0] - 2
    tiles, nocc = occ_ref.shape[:2]
    owned = nocc // wide_count
    pieces = even_ref.shape[0] + odd_ref.shape[0]
    width = vir_ref.shape[1] // pieces

    def fill(t, carry):
        block = part_refs[0][t].astype(jnp.float32)
        for ref in part_refs[1:]:
            block += ref[t].astype(jnp.float32)
        left = jnp.dot(
            occ_ref[t], block.astype(jnp.bfloat16), preferred_element_type=jnp.float32
        ).astype(jnp.bfloat16)
        lanes = pl.ds(pl.multiple_of(t * BLK, BLK), BLK)
        for q in range(wide_count):
            at = pl.multiple_of((wide_at ^ q) * owned, owned)
            left_ref[pl.ds(at, owned), lanes] = left[q * owned : (q + 1) * owned]
        return carry

    lax.fori_loop(0, tiles, fill, 0)
    for j in range(pieces):
        lanes = pl.ds(pl.multiple_of((narrow_at ^ j) * width, width), width)
        value = jnp.dot(left_ref[...], vir_ref[:, lanes], preferred_element_type=jnp.float32)
        if j % 2:
            odd_ref[j // 2] = value.astype(jnp.bfloat16)
        else:
            even_ref[j // 2] = value


def project_call(where, part_list, occ_sel, vir_sel, narrow_count):
    _, nocc = occ_sel.shape[:2]
    depth, nvir = vir_sel.shape
    shape = (narrow_count // 2, nocc, nvir // narrow_count)
    return pl.pallas_call(
        functools.partial(project_kernel, len(part_list)),
        out_shape=[
            jax.ShapeDtypeStruct(shape, jnp.float32),
            jax.ShapeDtypeStruct(shape, jnp.bfloat16),
        ],
        in_specs=[SMEM] + [VMEM] * (len(part_list) + 2),
        out_specs=[VMEM] * 2,
        scratch_shapes=[pltpu.VMEM((nocc, depth), jnp.bfloat16)],
        compiler_params=pltpu.CompilerParams(vmem_limit_bytes=32 * 1024 * 1024),
        cost_estimate=pl.CostEstimate(
            flops=2_400_000_000, bytes_accessed=10_000_000, transcendentals=0
        ),
        name="project",
    )(where, *part_list, occ_sel, vir_sel)


def body(
    dens_tiles,
    tile_dest,
    tile_place,
    tile_rows,
    tile_cols,
    ao_values,
    point_count,
    weights,
    kernel_first,
    kernel_second,
    occ_coef,
    vir_coef,
):
    wide_count = lax.axis_size("wide")
    narrow_count = lax.axis_size("narrow")
    tile_count = dens_tiles.shape[0]
    nocc, nvir = occ_coef.shape[1], vir_coef.shape[1]
    halves = narrow_count // NBAT
    points = ao_values.shape[2] // halves
    line = wide_count // 2
    wide = lax.axis_index("wide")
    narrow = lax.axis_index("narrow")
    batch, half = narrow // halves, narrow % halves
    level = wide // 2

    def across(x, least=0, most=line - 1):
        pairs = [(i, i ^ 1) for i in range(wide_count) if least <= i // 2 <= most]
        return lax.ppermute(x, "wide", pairs)

    def upward(x, k):
        return lax.ppermute(
            x, "wide", [(i, i + 2) for i in range(wide_count - 2) if i // 2 >= k - 1]
        )

    def downward(x, k):
        return lax.ppermute(
            x, "wide", [(i, i - 2) for i in range(2, wide_count) if i // 2 <= line - k]
        )

    def beside(x, mask):
        return lax.ppermute(x, "narrow", [(i, i ^ mask) for i in range(narrow_count)])

    own = lax.dynamic_slice(
        ao_values, (batch, 0, half * points), (1, ao_values.shape[1], points)
    )[0]
    up, down = {0: own}, {0: own}
    own_beside = across(own)
    ao_stages = [[own, own_beside]]
    ao_places = [wide, wide ^ 1]
    tiles = dens_tiles.reshape(tile_count, FIELDS * BLK, BLK)
    for k in range(1, line):
        up[k] = upward(up[k - 1], k)
        down[k] = downward(down[k - 1], k)
        up_beside = across(up[k], least=k)
        down_beside = across(down[k], most=line - 1 - k)
        ao_stages.append([up[k], up_beside, down[k], down_beside])
        low_ok, high_ok = level >= k, level + k < line
        ao_places += [
            jnp.where(low_ok, wide - 2 * k, -1),
            jnp.where(low_ok, (wide - 2 * k) ^ 1, -1),
            jnp.where(high_ok, wide + 2 * k, -1),
            jnp.where(high_ok, (wide + 2 * k) ^ 1, -1),
        ]
    routes = jnp.stack([tile_dest, tile_place]).reshape(1, -1)
    routes = lax.all_to_all(
        jnp.broadcast_to(routes, (narrow_count, routes.shape[1])),
        "narrow",
        split_axis=0,
        concat_axis=0,
        tiled=True,
    )
    tiles, routes = lax.optimization_barrier((tiles, routes))
    tile_list = [tiles]
    mask = narrow_count // 2
    while mask:
        pairs = []
        for x in tile_list:
            pairs += [x, beside(x, mask)]
        tile_list = pairs
        mask //= 2

    routes = jnp.take(routes, narrow ^ jnp.arange(narrow_count), axis=0)
    routes = routes.reshape(narrow_count, 2, tile_count * TOP)
    dests, places = routes[:, 0].reshape(-1), routes[:, 1].reshape(-1)
    mine = places // (KB * KB) == batch
    rows = places % (KB * KB) // KB
    cols = places % KB
    offset = dests // 2 - level
    other = (dests ^ wide) & 1
    occ_sel = occ_coef.reshape(-1, BLK, nocc)[tile_rows].transpose(0, 2, 1)
    vir_sel = vir_coef.reshape(-1, BLK, nvir)[tile_cols].reshape(tile_count * BLK, nvir)
    stages = jnp.arange(line)[:, None]
    active = mine[None] & (jnp.abs(offset)[None] == stages)
    indices = jnp.where(stages > 0, other[None] + 2 * (offset > 0).astype(jnp.int32)[None], other)
    count = dests.shape[0]
    spots = jnp.arange(count)
    earlier = spots[None, :] < spots[:, None]
    rank = jnp.sum((active[:, None, :] & earlier[None]).astype(jnp.int32), axis=2)
    hit = active[:, None, :] & (rank[:, None, :] == spots[None, :, None])
    order = jnp.sum(jnp.where(hit, spots - count, 0), axis=2) + count
    sizes = jnp.sum(active.astype(jnp.int32), axis=1)
    fill = jnp.full((line, UNROLL), count, jnp.int32)
    order = jnp.concatenate([order, fill, sizes[:, None]], axis=1)

    def extend(x, value):
        return jnp.concatenate([x, jnp.full((1,), value, jnp.int32)])

    more_dests, more_rows, more_cols = extend(dests, wide_count), extend(rows, 0), extend(cols, 0)
    all_tiles = jnp.concatenate(tile_list, axis=0)
    order, occ_sel, vir_sel = lax.optimization_barrier((order, occ_sel, vir_sel))
    density = None
    for k in range(line):
        stage_order = order[k]
        if density is not None:
            stage_order, density = lax.optimization_barrier((stage_order, density))
        part = density_call(
            stage_order,
            extend(indices[k], 0),
            more_dests,
            more_rows,
            more_cols,
            ao_stages[k],
            all_tiles,
            wide_count,
        )
        density = part if density is None else density + part
    density = lax.all_to_all(density, "wide", split_axis=0, concat_axis=0, tiled=True)
    density = jnp.sum(density, axis=0)

    def here(x):
        return lax.dynamic_slice(x, (batch, half * points), (1, points))

    used = lax.dynamic_slice(point_count, (batch,), (1,))
    inside = (half * points + jnp.arange(points))[None, :] < used[:, None]
    scale = jnp.where(inside, here(weights), jnp.float32(0.0))
    first, second = here(kernel_first), here(kernel_second)
    product = jnp.stack([density[1] * density[2], density[0] * density[2], density[0] * density[1]])
    potential = (first * density + second * product) * scale
    potential = lax.all_to_all(
        jnp.broadcast_to(potential[None], (wide_count,) + potential.shape),
        "wide",
        split_axis=0,
        concat_axis=0,
        tiled=True,
    )
    ao_list = [x for stage in ao_stages for x in stage]
    held_places = jnp.stack(ao_places)
    kept = jnp.where(mine, dests, -1)
    where = jnp.concatenate([jnp.stack([wide, narrow]), jnp.zeros((wide_count,), jnp.int32)])

    half_count = narrow_count // 2
    far = block_call(
        half_count, half_count, held_places, kept, rows, cols, potential, ao_list, tile_count
    )

    def fold(groups):
        mask = 1
        while len(groups) > 1:
            groups = [
                [
                    (p.astype(jnp.float32) + beside(q, mask).astype(jnp.float32)).astype(
                        jnp.bfloat16
                    )
                    for p, q in zip(groups[i], groups[i + 1])
                ]
                for i in range(0, len(groups), 2)
            ]
            mask *= 2
        return groups[0]

    far_sum = fold(far)
    potential, far_sum = lax.optimization_barrier((potential, far_sum))
    far_parts = []
    for f in range(FIELDS):
        far_parts.append(beside(far_sum[f], half_count))
    far_sum = far_parts
    near = block_call(0, half_count, held_places, kept, rows, cols, potential, ao_list, tile_count)
    near_sum = fold(near)
    results = []
    for f in range(FIELDS):
        even, odd = project_call(where, [near_sum[f], far_sum[f]], occ_sel, vir_sel, narrow_count)
        mask = 1
        while True:
            received = beside(odd, mask)
            even = even + received.astype(jnp.float32)
            mask *= 2
            if mask == narrow_count:
                break
            even = even.reshape((-1, 2) + even.shape[1:])
            even, odd = even[:, 0], even[:, 1].astype(jnp.bfloat16)
        value = even.reshape(wide_count, nocc // wide_count, nvir // narrow_count)
        mask = 1
        while mask < wide_count:
            value = value.reshape((-1, 2) + value.shape[1:])
            sent = lax.ppermute(
                value[:, 1].astype(jnp.bfloat16),
                "wide",
                [(i, i ^ mask) for i in range(wide_count)],
            )
            value = value[:, 0] + sent.astype(jnp.float32)
            mask *= 2
        results.append(value[0])
    return jnp.stack(results)


def solution(mesh):
    in_specs = (
        P(("wide", "narrow"), None, None, None),
        P(("wide", "narrow"), None),
        P(("wide", "narrow"), None),
        P(("wide", "narrow")),
        P(("wide", "narrow")),
        P("wide", None, None),
        P("wide"),
        P("wide", None),
        P("wide", None),
        P("wide", None),
        P("wide", None),
        P("narrow", None),
    )
    out_specs = P(None, "wide", "narrow")

    return jax.shard_map(body, mesh=mesh, in_specs=in_specs, out_specs=out_specs, check_vma=False)
```
